32 devices in a mesh: group: 4 (over z), seq: 4 (over x, core), tensor: 2 (over y).
Axes of the slice: x: 2, y: 2, z: 4, core: 2. Of those that a mesh axis runs over, the one named last changes fastest.
Arguments:
- queries: bfloat16 [4, 1024, 4096], P('group', 'seq', 'tensor'), as said below
- suffix_kv: bfloat16 [4, 1024, 2048], P('group', 'seq', 'tensor'), may hold values from -15 to 15
- suffix_seg: int32 [4, 1024], P('group', 'seq'), may hold values from 0 to 3, never falling along the last dimension, each value on 1 to 512 neighbouring positions
- prefix_pool: bfloat16 [4, 64, 128, 2048], P('group', 'seq', None, 'tensor'), as said below
- page_table: int32 [2, 32], P(None, 'seq'), may hold values from 0 to 15, as said below
- owner: int32 [2], replicated, may hold values from 0 to 3, as said below
- group_of: int32 [4], P('group'), may hold values from 0 to 1, as said below
Outputs:
- attention: bfloat16 [4, 1024, 4096], P('group', 'seq', 'tensor')
The draws below stay inside these ranges and needn't reach their ends.
Inputs may be any that keep to these rules, and one draw needn't show every extreme that they name: `queries`: of order one except in a few rows, which may be as large as 10 in every entry. `prefix_pool`: entries of order 2.5. `page_table`: within a row, the 8 entries of each index of seq are distinct. `owner`: Distinct. `group_of`: every request group is served by exactly two group indices.
All inputs are finite; a program needn't handle non-finite values.
Results may differ from the reference program's by a relative error of at most 0.0044.
Values may be sent and summed in bfloat16 or wider, within the bound.
A program may use at most 128 MiB of HBM per device.

```python
import math
import jax
import jax.numpy as jnp
import numpy as np
from jax import lax

Q_HEADS = 32
KV_HEADS = 8
HEAD = 128
PAGE = 128
REQS = 4
PG_DEV = 8
POOL = 16
PREFIX = 4096
SUF = 1024
MOST = 512
RG = 2
N_GROUP = 4
N_SEQ = 4


def draw_queries(key, part):
    shape = (N_GROUP, SUF, Q_HEADS * HEAD)
    values = jnp.clip(jax.random.normal(jax.random.fold_in(key, 11), shape, jnp.float32), -6.0, 6.0)
    return values.astype(jnp.bfloat16)


def draw_prefix_pool(key, part):
    shape = (N_GROUP, N_SEQ * POOL, PAGE, KV_HEADS * 2 * HEAD)
    values = 2.5 * jnp.clip(jax.random.normal(jax.random.fold_in(key, 13), shape, jnp.float32), -6.0, 6.0)
    return values.astype(jnp.bfloat16)


def draw_page_table(key, part):

    def one_row(row_key):
        return jax.random.permutation(row_key, POOL)[:PG_DEV].astype(jnp.int32)

    def ends_row(row_key):
        inner = (1 + jax.random.permutation(jax.random.fold_in(row_key, 1), POOL - 2)[:PG_DEV - 2]).astype(jnp.int32)
        full_row = jnp.concatenate([jnp.array([0, POOL - 1], jnp.int32), inner])
        order = jax.random.permutation(jax.random.fold_in(row_key, 2), PG_DEV)
        return full_row[order].astype(jnp.int32)
    row_keys = jax.random.split(jax.random.fold_in(key, 21), RG * N_SEQ)
    drawn_rows = jax.vmap(one_row)(row_keys)
    first_row = ends_row(jax.random.fold_in(key, 22))
    row_ids = jnp.arange(RG * N_SEQ, dtype=jnp.int32)
    rows_all = jnp.where((row_ids == 0)[:, None], first_row[None, :], drawn_rows)
    return rows_all.reshape(RG, N_SEQ * PG_DEV).astype(jnp.int32)


def draw_owner(key, part):
    return jax.random.permutation(jax.random.fold_in(key, 31), N_GROUP)[:RG].astype(jnp.int32)


def draw_group_of(key, part):
    return (jax.random.permutation(jax.random.fold_in(key, 41), N_GROUP) // 2).astype(jnp.int32)


def steps_of(own_key, dims, cuts, low, high):
    def one(axis_at, shards_of):
        draws = jax.random.uniform(jax.random.fold_in(jax.random.fold_in(own_key, 6), axis_at), (shards_of,), jnp.float32, low / len(cuts), high / len(cuts))
        return jnp.repeat(jnp.exp(draws), dims[axis_at] // shards_of).reshape((-1,) + (1,) * (len(dims) - axis_at - 1))

    gain = one(*cuts[0])
    for cut in cuts[1:]:
        gain = gain * one(*cut)
    return gain


def length_profile(amount, total, reach, lean):
    portions = [(1 << 20) // math.isqrt(rank ** lean) + 1 for rank in range(2, amount + 1)]
    surplus, given = total - reach - (amount - 1), [1] * (amount - 1)
    while surplus > 0:
        free = [i for i in range(amount - 1) if given[i] < reach]
        pool, budget = sum([portions[i] for i in free]), surplus
        for i in free:
            extra = min(reach - given[i], max(1, budget * portions[i] // pool), surplus)
            given[i] = given[i] + extra
            surplus = surplus - extra
    return np.array([reach] + given)


def ragged(stream_key, number_of, total, bound, lean):
    if number_of == 2:
        one = jax.random.randint(stream_key, (), max(1, total - bound), min(bound, total - 1) + 1)
        return jnp.stack([one, total - one])
    tallies = jnp.asarray(length_profile(number_of, total, bound, lean), jnp.int32)
    couples = (number_of - 1) // 2
    source_of, receiver = tallies[1:1 + 2 * couples:2], tallies[2:2 + 2 * couples:2]
    margin = jnp.minimum(source_of - 1, bound - receiver)
    moved = jax.random.randint(jax.random.fold_in(stream_key, 1), (couples,), 0, 1 << 20) % (margin + 1)
    tallies = tallies.at[1:1 + 2 * couples:2].set(source_of - moved).at[2:2 + 2 * couples:2].set(receiver + moved)
    return tallies[jax.random.permutation(jax.random.fold_in(stream_key, 2), number_of)]


def bell_draw(own_key, dims, deviation, limit, cuts=(), kind=jnp.bfloat16):
    values = jax.random.normal(own_key, dims, jnp.float32) * deviation
    if len(cuts) > 0:
        values = steps_of(own_key, dims, cuts, -0.22, 0.18) * values
    return jnp.clip(values, min=-limit, max=limit).astype(kind)


def setup_inputs(seed: int = 0) -> dict:
    streams_of = jax.random.split(jax.random.key(seed), 8)
    return {
        "queries": draw_queries(jax.random.fold_in(streams_of[7], 71), 0),
        "suffix_kv": bell_draw(streams_of[1], (N_GROUP, SUF, KV_HEADS * 2 * HEAD), 2.5, 15.0, ((0, 4), (1, 4), (2, 2))),
        "suffix_seg": jax.vmap(lambda own: jnp.searchsorted(jnp.cumsum(ragged(own, REQS, SUF, MOST, 2)), jnp.arange(SUF), side="right"))(jax.random.split(streams_of[2], N_GROUP)).reshape((N_GROUP, SUF)).astype(jnp.int32),
        "prefix_pool": draw_prefix_pool(jax.random.fold_in(streams_of[7], 71), 0),
        "page_table": draw_page_table(jax.random.fold_in(streams_of[7], 71), 0),
        "owner": draw_owner(jax.random.fold_in(streams_of[7], 71), 0),
        "group_of": draw_group_of(jax.random.fold_in(streams_of[7], 71), 0),
    }


NEG_FILL = -1e+30

def reference(queries, suffix_kv, suffix_seg, prefix_pool, page_table, owner, group_of):
    row_width = prefix_pool.shape[-1]
    head_count = row_width // (2 * HEAD)
    group_size = queries.shape[-1] // (head_count * HEAD)
    scale = 1.0 / math.sqrt(HEAD)
    pool_all = prefix_pool.reshape(N_GROUP, N_SEQ, POOL, PAGE, row_width)

    def one_group(group_index):
        request = group_of[group_index]
        source = owner[request]
        slot_ids = page_table[request].reshape(N_SEQ, PG_DEV)
        owner_pool = pool_all[source]
        pages = jax.vmap(lambda pool_rows, slot_row: pool_rows[slot_row])(owner_pool, slot_ids)
        prefix_rows = pages.reshape(PREFIX, row_width)
        kv_rows = jnp.concatenate([prefix_rows, suffix_kv[group_index]], 0).reshape(-1, head_count, 2, HEAD)
        query_rows = queries[group_index].reshape(SUF, head_count, group_size, HEAD)
        segment = suffix_seg[group_index]
        position = jnp.arange(SUF, dtype=jnp.int32)
        suffix_seen = (segment[None, :] == segment[:, None]) & (position[None, :] <= position[:, None])
        visible = jnp.concatenate([jnp.ones((SUF, PREFIX), dtype=bool), suffix_seen], 1)

        def one_head(head_index):
            query_head = query_rows[:, head_index].astype(jnp.float32)
            key_head = kv_rows[:, head_index, 0].astype(jnp.float32)
            value_head = kv_rows[:, head_index, 1].astype(jnp.float32)
            scores = jnp.einsum('tgd,kd->tgk', query_head, key_head) * scale
            scores = jnp.where(visible[:, None, :], scores, NEG_FILL)
            row_max = lax.optimization_barrier(jnp.max(scores, axis=-1, keepdims=True))
            weights = jnp.where(visible[:, None, :], jnp.exp(scores - row_max), 0.0)
            totals = lax.optimization_barrier(jnp.sum(weights, axis=-1, keepdims=True))
            weights_b = lax.optimization_barrier(weights.astype(jnp.bfloat16))
            context = jnp.einsum('tgk,kd->tgd', weights_b.astype(jnp.float32), value_head)
            return context / totals
        heads_out = lax.map(one_head, jnp.arange(head_count))
        return heads_out.transpose(1, 0, 2, 3).reshape(SUF, -1).astype(jnp.bfloat16)
    return lax.map(one_group, jnp.arange(N_GROUP))
```

```python
import functools
import math

import jax
import jax.numpy as jnp
from jax import lax
from jax.experimental import pallas as pl
from jax.experimental.pallas import tpu as pltpu
from jax.sharding import PartitionSpec as P

HEAD = 128


NEG_FILL = -1e30


def broadcast(value, axis, root):
    mine = lax.axis_index(axis) == root
    return lax.psum(jnp.where(mine, value, jnp.zeros_like(value)), axis)


def absorb(carried, query_rows, key_block, valid):
    running_max, running_sum, accumulator = carried
    scale = 1.0 / math.sqrt(HEAD)
    key_rows = key_block[:, :, 0, :]
    value_rows = key_block[:, :, 1, :]
    scores = (
        jnp.einsum("thgd,khd->htgk", query_rows, key_rows, preferred_element_type=jnp.float32)
        * scale
    )
    if valid is not None:
        scores = jnp.where(valid[None, :, None, :], scores, NEG_FILL)
    new_max = jnp.maximum(running_max, jnp.max(scores, axis=-1, keepdims=True))
    weight = jnp.exp(scores - new_max)
    if valid is not None:
        weight = jnp.where(valid[None, :, None, :], weight, 0.0)
    factor = jnp.exp(running_max - new_max)
    running_sum = running_sum * factor + jnp.sum(weight, axis=-1, keepdims=True)
    accumulator = accumulator * factor + jnp.einsum(
        "htgk,khd->htgd",
        weight.astype(jnp.bfloat16),
        value_rows,
        preferred_element_type=jnp.float32,
    )
    return (new_max, running_sum, accumulator)


def sweep(carried, query_rows, kv_rows, mask_for):
    row_count = kv_rows.shape[0]
    block_rows = math.gcd(row_count, 1024)
    head_count = kv_rows.shape[1] // (2 * HEAD)

    def absorb_block(block_index, state_now):
        offset = block_index * block_rows
        key_block = lax.dynamic_slice_in_dim(kv_rows, offset, block_rows, 0).reshape(
            block_rows, head_count, 2, HEAD
        )
        return absorb(state_now, query_rows, key_block, mask_for(offset, block_rows))

    if row_count == block_rows:
        return absorb_block(0, carried)
    return lax.fori_loop(0, row_count // block_rows, absorb_block, carried)


def combine(earlier, later):
    new_max = jnp.maximum(earlier[0], later[0])
    scale_first = jnp.exp(earlier[0] - new_max)
    scale_second = jnp.exp(later[0] - new_max)
    return (
        new_max,
        earlier[1] * scale_first + later[1] * scale_second,
        earlier[2] * scale_first + later[2] * scale_second,
    )


def no_mask(offset, block_rows):
    return None


def local(queries, suffix_kv, suffix_seg, prefix_pool, page_table, owner, group_of):
    tokens = queries.shape[1]
    row_width = suffix_kv.shape[-1]
    head_count = row_width // (2 * HEAD)
    group_size = queries.shape[-1] // (head_count * HEAD)
    query_rows = queries[0].reshape(tokens, head_count, group_size, HEAD)
    page_pool = prefix_pool[0]
    my_group = group_of[0]
    held_shape = (page_table.shape[1] * page_pool.shape[1], row_width)

    def compact(slot_ids):
        return jnp.take(page_pool, slot_ids, axis=0).reshape(-1, row_width)

    def visit_group(request, held_pages):
        moved_pages = broadcast(compact(page_table[request]), "group", owner[request])
        return jnp.where(request == my_group, moved_pages, held_pages)

    prefix_rows = lax.fori_loop(
        0, page_table.shape[0], visit_group, jnp.zeros(held_shape, jnp.bfloat16)
    )
    fresh_state = (
        jnp.full((head_count, tokens, group_size, 1), NEG_FILL, jnp.float32),
        jnp.zeros((head_count, tokens, group_size, 1), jnp.float32),
        jnp.zeros((head_count, tokens, group_size, HEAD), jnp.float32),
    )
    before = sweep(
        fresh_state, query_rows, lax.all_gather(prefix_rows, "seq", axis=0, tiled=True), no_mask
    )
    first_row = lax.axis_index("seq") * tokens
    query_pos = first_row + jnp.arange(tokens, dtype=jnp.int32)
    query_seg = suffix_seg[0]
    first_index = jnp.int32(0)
    kv_rows = lax.all_gather(suffix_kv[0], "seq", axis=0, tiled=True)
    key_segments = lax.all_gather(suffix_seg[0], "seq", axis=0, tiled=True)

    def mask_for(offset, block_rows):
        block_seg = lax.dynamic_slice_in_dim(key_segments, offset, block_rows, 0)
        key_pos = first_index + offset + jnp.arange(block_rows, dtype=jnp.int32)
        return (block_seg[None, :] == query_seg[:, None]) & (key_pos[None, :] <= query_pos[:, None])

    combined = sweep(fresh_state, query_rows, kv_rows, mask_for)
    final_state = combine(before, combined)
    outcome = final_state[2] / final_state[1]
    return outcome.transpose(1, 0, 2, 3).reshape(1, tokens, -1).astype(jnp.bfloat16)

MESH = pl.DeviceIdType.MESH
EXP2_SCALE = math.log2(math.e) / math.sqrt(HEAD)


def page_kernel(slots_ref, pool_ref, out_ref):
    for h in range(out_ref.shape[0]):
        out_ref[h] = pool_ref[0, :, h * 2 * HEAD : (h + 1) * 2 * HEAD]


def own_pages(pool, slots):
    page, width = pool.shape[1:]
    heads, count = width // (2 * HEAD), slots.shape[0]
    return pl.pallas_call(
        page_kernel,
        grid_spec=pltpu.PrefetchScalarGridSpec(
            num_scalar_prefetch=1,
            grid=(count,),
            in_specs=[pl.BlockSpec((1, page, width), lambda j, slots: (slots[j], 0, 0))],
            out_specs=pl.BlockSpec((heads, page, 2 * HEAD), lambda j, slots: (0, j, 0)),
        ),
        out_shape=jax.ShapeDtypeStruct((heads, count * page, 2 * HEAD), pool.dtype),
    )(slots, pool)


def choose(flag, first, second):
    return lax.select(flag != 0, first, second)


def fused_kernel(
    lanes, heads, group_size,
    flags, queries, qseg, own, suffix, seg,
    out,
    right_in, left_in, right_out, left_out, kv, skv, sseg, m_ref, l_ref, acc,
    sem_right_s, sem_right_r, sem_left_s, sem_left_r,
    sem_core_s, sem_core_r, sem_x_s, sem_x_r, sem_f_s, sem_f_r,
    sem_suf_s, sem_suf_r, sem_seg_s, sem_seg_r,
):
    z = lax.axis_index("group")
    s = lax.axis_index("seq")
    chunks, rows = own.shape[:2]
    halves = chunks // heads
    tokens = queries.shape[0]
    partner = s + 1 - 2 * lax.rem(s, 2)
    across = lax.rem(s + 2, 4)
    across_partner = lax.rem(partner + 2, 4)
    mid = (z == 1) | (z == 2)

    barrier = pltpu.get_barrier_semaphore()
    for there in (partner, across):
        pl.semaphore_signal(barrier, inc=1, device_id={"seq": there}, device_id_type=MESH)

    @pl.when(z > 0)
    def _():
        pl.semaphore_signal(barrier, inc=1, device_id={"group": z - 1}, device_id_type=MESH)

    @pl.when(z < 3)
    def _():
        pl.semaphore_signal(barrier, inc=1, device_id={"group": z + 1}, device_id_type=MESH)

    pl.semaphore_wait(barrier, jnp.where(mid, 4, 3))

    def move(src, dst, send, recv, axis, there):
        return pltpu.make_async_remote_copy(
            src_ref=src, dst_ref=dst, send_sem=send, recv_sem=recv,
            device_id={axis: there}, device_id_type=MESH,
        )

    def right(lane, k, src=None):
        return move(
            right_out.at[lane, k] if src is None else src, right_in.at[lane, k],
            sem_right_s.at[lane, k], sem_right_r.at[lane, k], "group", lax.rem(z + 1, 4),
        )

    def left(lane, k, src=None):
        return move(
            left_out.at[lane, k] if src is None else src, left_in.at[lane, k],
            sem_left_s.at[lane, k], sem_left_r.at[lane, k], "group", lax.rem(z + 3, 4),
        )

    def core(k):
        return move(kv.at[0, k], kv.at[1, k], sem_core_s.at[k], sem_core_r.at[k], "seq", partner)

    def cross(k):
        return move(kv.at[0, k], kv.at[2, k], sem_x_s.at[k], sem_x_r.at[k], "seq", across)

    def forward(k):
        return move(kv.at[2, k], kv.at[3, k], sem_f_s.at[k], sem_f_r.at[k], "seq", partner)

    def suffix_copies(j):
        src_kv, src_seg = (suffix, seg) if j < 3 else (skv.at[1], sseg.at[1])
        there = across if j == 2 else partner
        slot = {1: 0, 2: 1, 3: 2}[j]
        return (
            move(src_kv, skv.at[slot], sem_suf_s.at[slot], sem_suf_r.at[slot], "seq", there),
            move(src_seg, sseg.at[slot], sem_seg_s.at[slot], sem_seg_r.at[slot], "seq", there),
        )

    @pl.when(z == 0)
    def _():
        @pl.loop(0, chunks)
        def _(k):
            right(0, k, own.at[k]).start()

    @pl.when(z == 3)
    def _():
        @pl.loop(0, chunks)
        def _(k):
            left(0, k, own.at[k]).start()

    for j in (2, 1):
        for c in suffix_copies(j):
            c.start()

    def attend(h, blocks, init):
        def one(i, carry):
            head = h * group_size + i
            col = pl.multiple_of(head * HEAD, HEAD)
            q = queries[:, pl.ds(col, HEAD)]
            scores = []
            for keys, _, valid in blocks:
                sc = lax.dot_general(
                    q, keys(), (((1,), (1,)), ((), ())), preferred_element_type=jnp.float32
                )
                if valid is not None:
                    sc = jnp.where(valid, sc, NEG_FILL)
                scores.append(sc)
            top = jnp.max(scores[0], axis=1, keepdims=True)
            for sc in scores[1:]:
                top = jnp.maximum(top, jnp.max(sc, axis=1, keepdims=True))
            if not init:
                old = m_ref[head][:, :1]
                top = jnp.maximum(old, top)
                factor = jnp.exp2((old - top) * EXP2_SCALE)
            total, context = None, None
            for sc, (_, values, valid) in zip(scores, blocks):
                w = jnp.exp2((sc - top) * EXP2_SCALE)
                if valid is not None:
                    w = jnp.where(valid, w, 0.0)
                part = jnp.sum(w, axis=1, keepdims=True)
                add = jnp.dot(
                    w.astype(jnp.bfloat16), values(), preferred_element_type=jnp.float32
                )
                total = part if total is None else total + part
                context = add if context is None else context + add
            if not init:
                total = total + l_ref[head][:, :1] * factor
                context = context + acc[head] * factor
            m_ref[head] = jnp.broadcast_to(top, (tokens, HEAD))
            l_ref[head] = jnp.broadcast_to(total, (tokens, HEAD))
            acc[head] = context
            return carry

        lax.fori_loop(0, group_size, one, 0)

    def attend_suffix():
        q_pos = s * tokens + lax.broadcasted_iota(jnp.int32, (tokens, tokens), 0)
        k_off = lax.broadcasted_iota(jnp.int32, (tokens, tokens), 1)
        q_seg = qseg[:, :1]

        def mask(seg_rows, origin):
            return (seg_rows == q_seg) & (origin * tokens + k_off <= q_pos)

        sources = (
            (suffix, seg, s), (skv.at[0], sseg.at[0], partner),
            (skv.at[1], sseg.at[1], across), (skv.at[2], sseg.at[2], across_partner),
        )
        masks = [mask(sg[:1, :], origin) for _, sg, origin in sources]

        @pl.loop(0, heads)
        def _(h):
            base = pl.multiple_of(h * 2 * HEAD, HEAD)
            attend(h, [
                (
                    lambda ref=ref: ref[:, pl.ds(base, HEAD)],
                    lambda ref=ref: ref[:, pl.ds(pl.multiple_of(base + HEAD, HEAD), HEAD)],
                    valid,
                )
                for (ref, _, _), valid in zip(sources, masks)
            ], True)

    def attend_prefix(k):
        attend(k // halves, [
            (lambda j=j: kv[j, k, :, :HEAD], lambda j=j: kv[j, k, :, HEAD:], None)
            for j in range(4)
        ], False)

    depth = jnp.maximum(z, 3 - z)

    def step(i, carry):
        k_right = i - z

        @pl.when(mid & (k_right >= 0) & (k_right < chunks))
        def _():
            k = k_right

            @pl.when(z == 1)
            def _():
                right(0, k).wait_recv()
                for lane in range(lanes):
                    right_out[lane, k] = choose(flags[0 + lane], own[k], right_in[0, k])
                    right(lane, k).start()

            @pl.when(z == 2)
            def _():
                got = None
                for lane in range(lanes):
                    right(lane, k).wait_recv()
                got = right_in[0, k]
                if lanes > 1:
                    got = choose(flags[4], right_in[1, k], got)
                right_out[0, k] = choose(flags[0], own[k], got)
                right(0, k).start()

        k_left = i - (3 - z)

        @pl.when(mid & (k_left >= 0) & (k_left < chunks))
        def _():
            k = k_left

            @pl.when(z == 2)
            def _():
                left(0, k).wait_recv()
                for lane in range(lanes):
                    left_out[lane, k] = choose(flags[2 + lane], own[k], left_in[0, k])
                    left(lane, k).start()

            @pl.when(z == 1)
            def _():
                for lane in range(lanes):
                    left(lane, k).wait_recv()
                got = left_in[0, k]
                if lanes > 1:
                    got = choose(flags[5], left_in[1, k], got)
                left_out[0, k] = choose(flags[2], own[k], got)
                left(0, k).start()

        k_mine = i - depth

        @pl.when((k_mine >= 0) & (k_mine < chunks))
        def _():
            k = k_mine

            @pl.when(z == 0)
            def _():
                left(0, k).wait_recv()
                kv[0, k] = choose(flags[6], own[k], left_in[0, k])

            @pl.when(z == 3)
            def _():
                right(0, k).wait_recv()
                kv[0, k] = choose(flags[6], own[k], right_in[0, k])

            @pl.when(z == 1)
            def _():
                came = left_in[0, k]
                if lanes > 1:
                    came = choose(flags[8], left_in[1, k], came)
                came = choose(flags[7], right_in[0, k], came)
                kv[0, k] = choose(flags[6], own[k], came)

            @pl.when(z == 2)
            def _():
                came = right_in[0, k]
                if lanes > 1:
                    came = choose(flags[8], right_in[1, k], came)
                came = choose(flags[7], came, left_in[0, k])
                kv[0, k] = choose(flags[6], own[k], came)

            cross(k).start()
            core(k).start()

        k_cross = i - depth - 1

        @pl.when((k_cross >= 0) & (k_cross < chunks))
        def _():
            cross(k_cross).wait_recv()
            forward(k_cross).start()

        k_use = i - depth - 2

        @pl.when((k_use >= 0) & (k_use < chunks))
        def _():
            core(k_use).wait_recv()
            forward(k_use).wait_recv()
            attend_prefix(k_use)

        @pl.when(i == 1)
        def _():
            for c in suffix_copies(2):
                c.wait_recv()
            for c in suffix_copies(3):
                c.start()
            for j in (1, 3):
                for c in suffix_copies(j):
                    c.wait_recv()
            attend_suffix()

        return carry

    lax.fori_loop(0, chunks + depth + 2, step, 0)

    @pl.loop(0, heads * group_size)
    def _(head):
        col = pl.multiple_of(head * HEAD, HEAD)
        out[:, pl.ds(col, HEAD)] = (acc[head] / l_ref[head]).astype(out.dtype)

    for j in (1, 2, 3):
        for c in suffix_copies(j):
            c.wait_send()

    @pl.loop(0, chunks)
    def _(k):
        core(k).wait_send()
        cross(k).wait_send()
        forward(k).wait_send()

        @pl.when(z < 3)
        def _():
            right(0, k).wait_send()

        @pl.when(z > 0)
        def _():
            left(0, k).wait_send()

        if lanes > 1:
            @pl.when(z == 1)
            def _():
                right(1, k).wait_send()

            @pl.when(z == 2)
            def _():
                left(1, k).wait_send()


def fused(lanes, flags, queries, qseg, own, suffix, seg):
    tokens, width = queries.shape
    heads = suffix.shape[1] // (2 * HEAD)
    q_heads = width // HEAD
    chunks, rows = own.shape[:2]
    piece = (rows, 2 * HEAD)
    vmem = pl.BlockSpec(memory_space=pltpu.VMEM)
    dma = pltpu.SemaphoreType.DMA
    return pl.pallas_call(
        functools.partial(fused_kernel, lanes, heads, q_heads // heads),
        out_shape=jax.ShapeDtypeStruct((tokens, width), jnp.bfloat16),
        in_specs=[pl.BlockSpec(memory_space=pltpu.SMEM)] + [vmem] * 5,
        out_specs=vmem,
        scratch_shapes=[
            pltpu.VMEM((lanes, chunks) + piece, jnp.bfloat16),
            pltpu.VMEM((lanes, chunks) + piece, jnp.bfloat16),
            pltpu.VMEM((lanes, chunks) + piece, jnp.bfloat16),
            pltpu.VMEM((lanes, chunks) + piece, jnp.bfloat16),
            pltpu.VMEM((4, chunks) + piece, jnp.bfloat16),
            pltpu.VMEM((3,) + suffix.shape, jnp.bfloat16),
            pltpu.VMEM((3,) + seg.shape, jnp.int32),
            pltpu.VMEM((q_heads, tokens, HEAD), jnp.float32),
            pltpu.VMEM((q_heads, tokens, HEAD), jnp.float32),
            pltpu.VMEM((q_heads, tokens, HEAD), jnp.float32),
        ]
        + [dma((lanes, chunks))] * 4
        + [dma((chunks,))] * 6
        + [dma((3,))] * 4,
        compiler_params=pltpu.CompilerParams(
            collective_id=lanes, has_side_effects=True, vmem_limit_bytes=58 << 20
        ),
    )(flags, queries, qseg, own, suffix, seg)


def local_fused(queries, suffix_kv, suffix_seg, prefix_pool, page_table, owner, group_of):
    z = lax.axis_index("group")
    wants = lax.all_gather(group_of, "group", axis=0, tiled=True)
    owner_of = owner[wants]
    mine_of = owner[group_of[0]]
    slots = lax.dynamic_index_in_dim(
        page_table, jnp.where(owner[1] == z, 1, 0), 0, keepdims=False
    )
    own = own_pages(prefix_pool[0], slots)
    own = own.reshape(-1, own.shape[1] // 2, own.shape[2])
    seg = jnp.broadcast_to(suffix_seg, (8, suffix_seg.shape[1]))
    qseg = jnp.broadcast_to(suffix_seg[0][:, None], (suffix_seg.shape[1], HEAD))

    two = ((owner[0] < 2) & (owner[1] < 2) & (wants[2] != wants[3])) | (
        (owner[0] >= 2) & (owner[1] >= 2) & (wants[0] != wants[1])
    )
    lane = lambda r: r == 1

    def call(lanes):
        need_right = jnp.where(owner_of[2] < 2, owner_of[2], owner_of[3])
        need_left = jnp.where(owner_of[1] >= 2, owner_of[1], owner_of[0])
        if lanes == 1:
            r1 = need_right == 1
            l2 = need_left == 2
            right0 = jnp.where(z == 1, r1, owner_of[3] == 2)
            left0 = jnp.where(z == 2, l2, owner_of[0] == 1)
            right1 = left1 = jnp.bool_(False)
        else:
            right0 = jnp.where(z == 1, owner[0] == 1, owner_of[3] == 2)
            left0 = jnp.where(z == 2, owner[0] == 2, owner_of[0] == 1)
            right1, left1 = owner[1] == 1, owner[1] == 2
        flags = jnp.stack([
            right0, right1, left0, left1, lane(wants[3]), lane(wants[0]),
            mine_of == z, mine_of < z, lane(group_of[0]),
        ]).astype(jnp.int32)
        return fused(lanes, flags, queries[0], qseg, own, suffix_kv[0], seg)

    return lax.cond(two, lambda: call(2), lambda: call(1))[None]


def fits(mesh):
    return dict(mesh.shape) == {"group": 4, "seq": 4, "tensor": 2}


def solution(mesh):
    return jax.shard_map(
        local_fused if fits(mesh) else local,
        mesh=mesh,
        in_specs=(
            P("group", "seq", "tensor"),
            P("group", "seq", "tensor"),
            P("group", "seq"),
            P("group", "seq", None, "tensor"),
            P(None, "seq"),
            P(),
            P("group"),
        ),
        out_specs=P("group", "seq", "tensor"),
        check_vma=False,
    )
```

```python
import functools
import math

import jax
import jax.numpy as jnp
from jax import lax
from jax.experimental import pallas as pl
from jax.experimental.pallas import tpu as pltpu
from jax.sharding import PartitionSpec as P

HEAD = 128


NEG_FILL = -1e30


def broadcast(value, axis, root):
    mine = lax.axis_index(axis) == root
    return lax.psum(jnp.where(mine, value, jnp.zeros_like(value)), axis)


def absorb(carried, query_rows, key_block, valid):
    running_max, running_sum, accumulator = carried
    scale = 1.0 / math.sqrt(HEAD)
    key_rows = key_block[:, :, 0, :]
    value_rows = key_block[:, :, 1, :]
    scores = (
        jnp.einsum("thgd,khd->htgk", query_rows, key_rows, preferred_element_type=jnp.float32)
        * scale
    )
    if valid is not None:
        scores = jnp.where(valid[None, :, None, :], scores, NEG_FILL)
    new_max = jnp.maximum(running_max, jnp.max(scores, axis=-1, keepdims=True))
    weight = jnp.exp(scores - new_max)
    if valid is not None:
        weight = jnp.where(valid[None, :, None, :], weight, 0.0)
    factor = jnp.exp(running_max - new_max)
    running_sum = running_sum * factor + jnp.sum(weight, axis=-1, keepdims=True)
    accumulator = accumulator * factor + jnp.einsum(
        "htgk,khd->htgd",
        weight.astype(jnp.bfloat16),
        value_rows,
        preferred_element_type=jnp.float32,
    )
    return (new_max, running_sum, accumulator)


def sweep(carried, query_rows, kv_rows, mask_for):
    row_count = kv_rows.shape[0]
    block_rows = math.gcd(row_count, 1024)
    head_count = kv_rows.shape[1] // (2 * HEAD)

    def absorb_block(block_index, state_now):
        offset = block_index * block_rows
        key_block = lax.dynamic_slice_in_dim(kv_rows, offset, block_rows, 0).reshape(
            block_rows, head_count, 2, HEAD
        )
        return absorb(state_now, query_rows, key_block, mask_for(offset, block_rows))

    if row_count == block_rows:
        return absorb_block(0, carried)
    return lax.fori_loop(0, row_count // block_rows, absorb_block, carried)


def combine(earlier, later):
    new_max = jnp.maximum(earlier[0], later[0])
    scale_first = jnp.exp(earlier[0] - new_max)
    scale_second = jnp.exp(later[0] - new_max)
    return (
        new_max,
        earlier[1] * scale_first + later[1] * scale_second,
        earlier[2] * scale_first + later[2] * scale_second,
    )


def no_mask(offset, block_rows):
    return None


def local(queries, suffix_kv, suffix_seg, prefix_pool, page_table, owner, group_of):
    tokens = queries.shape[1]
    row_width = suffix_kv.shape[-1]
    head_count = row_width // (2 * HEAD)
    group_size = queries.shape[-1] // (head_count * HEAD)
    query_rows = queries[0].reshape(tokens, head_count, group_size, HEAD)
    page_pool = prefix_pool[0]
    my_group = group_of[0]
    held_shape = (page_table.shape[1] * page_pool.shape[1], row_width)

    def compact(slot_ids):
        return jnp.take(page_pool, slot_ids, axis=0).reshape(-1, row_width)

    def visit_group(request, held_pages):
        moved_pages = broadcast(compact(page_table[request]), "group", owner[request])
        return jnp.where(request == my_group, moved_pages, held_pages)

    prefix_rows = lax.fori_loop(
        0, page_table.shape[0], visit_group, jnp.zeros(held_shape, jnp.bfloat16)
    )
    fresh_state = (
        jnp.full((head_count, tokens, group_size, 1), NEG_FILL, jnp.float32),
        jnp.zeros((head_count, tokens, group_size, 1), jnp.float32),
        jnp.zeros((head_count, tokens, group_size, HEAD), jnp.float32),
    )
    before = sweep(
        fresh_state, query_rows, lax.all_gather(prefix_rows, "seq", axis=0, tiled=True), no_mask
    )
    first_row = lax.axis_index("seq") * tokens
    query_pos = first_row + jnp.arange(tokens, dtype=jnp.int32)
    query_seg = suffix_seg[0]
    first_index = jnp.int32(0)
    kv_rows = lax.all_gather(suffix_kv[0], "seq", axis=0, tiled=True)
    key_segments = lax.all_gather(suffix_seg[0], "seq", axis=0, tiled=True)

    def mask_for(offset, block_rows):
        block_seg = lax.dynamic_slice_in_dim(key_segments, offset, block_rows, 0)
        key_pos = first_index + offset + jnp.arange(block_rows, dtype=jnp.int32)
        return (block_seg[None, :] == query_seg[:, None]) & (key_pos[None, :] <= query_pos[:, None])

    combined = sweep(fresh_state, query_rows, kv_rows, mask_for)
    final_state = combine(before, combined)
    outcome = final_state[2] / final_state[1]
    return outcome.transpose(1, 0, 2, 3).reshape(1, tokens, -1).astype(jnp.bfloat16)

MESH = pl.DeviceIdType.MESH
EXP2_SCALE = math.log2(math.e) / math.sqrt(HEAD)


def choose(flag, first, second):
    return lax.select(flag != 0, first, second)


def fused_kernel(
    lanes, heads, group_size,
    owner, group_of, pages, queries, suffix, seg_row, pool,
    out,
    own, seg, qseg, wants, wanted,
    right_in, left_in, right_out, left_out, kv, skv, sseg, m_ref, l_ref, acc,
    sem_right_s, sem_right_r, sem_left_s, sem_left_r,
    sem_core_s, sem_core_r, sem_x_s, sem_x_r, sem_f_s, sem_f_r,
    sem_suf_s, sem_suf_r, sem_seg_s, sem_seg_r, sem_want_s, sem_want_r,
):
    z = lax.axis_index("group")
    s = lax.axis_index("seq")
    chunks, rows = own.shape[:2]
    halves = chunks // heads
    tokens = queries.shape[0]
    partner = s + 1 - 2 * lax.rem(s, 2)
    across = lax.rem(s + 2, 4)
    across_partner = lax.rem(partner + 2, 4)
    mid = (z == 1) | (z == 2)

    owner_0, owner_1, want = owner[0], owner[1], group_of[0]
    owner_mine = jnp.where(want == 1, owner_1, owner_0)

    wanted[...] = jnp.zeros_like(wanted)
    barrier = pltpu.get_barrier_semaphore()
    for there in (partner, across):
        pl.semaphore_signal(barrier, inc=1, device_id={"seq": there}, device_id_type=MESH)

    @pl.when(z > 0)
    def _():
        pl.semaphore_signal(barrier, inc=1, device_id={"group": z - 1}, device_id_type=MESH)

    @pl.when(z < 3)
    def _():
        pl.semaphore_signal(barrier, inc=1, device_id={"group": z + 1}, device_id_type=MESH)

    wants[...] = jnp.broadcast_to(want, wants.shape)
    seg[...] = jnp.broadcast_to(seg_row[...], seg.shape)
    qseg[...] = jnp.broadcast_to(seg_row[...], (HEAD, tokens)).T

    owned = jnp.where(owner_1 == z, 1, 0)
    page = pool.shape[1]
    in_half = rows // page

    @pl.loop(0, pages.shape[1])
    def _(j):
        slot = pages[owned, j]
        place = pl.ds(pl.multiple_of(lax.rem(j, in_half) * page, page), page)
        for h in range(heads):
            own[h * halves + j // in_half, place, :] = pool[
                slot, :, h * 2 * HEAD : (h + 1) * 2 * HEAD
            ]

    pl.semaphore_wait(barrier, jnp.where(mid, 4, 3))

    def move(src, dst, send, recv, axis, there):
        return pltpu.make_async_remote_copy(
            src_ref=src, dst_ref=dst, send_sem=send, recv_sem=recv,
            device_id={axis: there}, device_id_type=MESH,
        )

    def right(lane, k, src=None):
        return move(
            right_out.at[lane, k] if src is None else src, right_in.at[lane, k],
            sem_right_s.at[lane, k], sem_right_r.at[lane, k], "group", lax.rem(z + 1, 4),
        )

    def left(lane, k, src=None):
        return move(
            left_out.at[lane, k] if src is None else src, left_in.at[lane, k],
            sem_left_s.at[lane, k], sem_left_r.at[lane, k], "group", lax.rem(z + 3, 4),
        )

    def core(k):
        return move(kv.at[0, k], kv.at[1, k], sem_core_s.at[k], sem_core_r.at[k], "seq", partner)

    def cross(k):
        return move(kv.at[0, k], kv.at[2, k], sem_x_s.at[k], sem_x_r.at[k], "seq", across)

    def forward(k):
        return move(kv.at[2, k], kv.at[3, k], sem_f_s.at[k], sem_f_r.at[k], "seq", partner)

    def suffix_copies(j):
        src_kv, src_seg = (suffix, seg) if j < 3 else (skv.at[1], sseg.at[1])
        there = across if j == 2 else partner
        slot = {1: 0, 2: 1, 3: 2}[j]
        return (
            move(src_kv, skv.at[slot], sem_suf_s.at[slot], sem_suf_r.at[slot], "seq", there),
            move(src_seg, sseg.at[slot], sem_seg_s.at[slot], sem_seg_r.at[slot], "seq", there),
        )

    def want_copy(there):
        return move(wants, wanted, sem_want_s, sem_want_r, "group", there)

    @pl.when((z == 0) | (z == 3))
    def _():
        want_copy(jnp.where(z == 0, 1, 2)).start()

    @pl.when(z == 0)
    def _():
        @pl.loop(0, chunks)
        def _(k):
            right(0, k, own.at[k]).start()

    @pl.when(z == 3)
    def _():
        @pl.loop(0, chunks)
        def _(k):
            left(0, k, own.at[k]).start()

    for j in (2, 1):
        for c in suffix_copies(j):
            c.start()

    def attend(h, blocks, init):
        def one(i, carry):
            head = h * group_size + i
            col = pl.multiple_of(head * HEAD, HEAD)
            q = queries[:, pl.ds(col, HEAD)]
            scores = []
            for keys, _, valid in blocks:
                sc = lax.dot_general(
                    q, keys(), (((1,), (1,)), ((), ())), preferred_element_type=jnp.float32
                )
                if valid is not None:
                    sc = jnp.where(valid, sc, NEG_FILL)
                scores.append(sc)
            top = jnp.max(scores[0], axis=1, keepdims=True)
            for sc in scores[1:]:
                top = jnp.maximum(top, jnp.max(sc, axis=1, keepdims=True))
            if not init:
                old = m_ref[head][:, :1]
                top = jnp.maximum(old, top)
                factor = jnp.exp2((old - top) * EXP2_SCALE)
            total, context = None, None
            for sc, (_, values, valid) in zip(scores, blocks):
                w = jnp.exp2((sc - top) * EXP2_SCALE)
                if valid is not None:
                    w = jnp.where(valid, w, 0.0)
                part = jnp.sum(w, axis=1, keepdims=True)
                add = jnp.dot(
                    w.astype(jnp.bfloat16), values(), preferred_element_type=jnp.float32
                )
                total = part if total is None else total + part
                context = add if context is None else context + add
            if not init:
                total = total + l_ref[head][:, :1] * factor
                context = context + acc[head] * factor
            m_ref[head] = jnp.broadcast_to(top, (tokens, HEAD))
            l_ref[head] = jnp.broadcast_to(total, (tokens, HEAD))
            acc[head] = context
            return carry

        lax.fori_loop(0, group_size, one, 0)

    def attend_suffix():
        q_pos = s * tokens + lax.broadcasted_iota(jnp.int32, (tokens, tokens), 0)
        k_off = lax.broadcasted_iota(jnp.int32, (tokens, tokens), 1)
        q_seg = qseg[:, :1]

        def mask(seg_rows, origin):
            return (seg_rows == q_seg) & (origin * tokens + k_off <= q_pos)

        sources = (
            (suffix, seg, s), (skv.at[0], sseg.at[0], partner),
            (skv.at[1], sseg.at[1], across), (skv.at[2], sseg.at[2], across_partner),
        )
        masks = [mask(sg[:1, :], origin) for _, sg, origin in sources]

        @pl.loop(0, heads)
        def _(h):
            base = pl.multiple_of(h * 2 * HEAD, HEAD)
            attend(h, [
                (
                    lambda ref=ref: ref[:, pl.ds(base, HEAD)],
                    lambda ref=ref: ref[:, pl.ds(pl.multiple_of(base + HEAD, HEAD), HEAD)],
                    valid,
                )
                for (ref, _, _), valid in zip(sources, masks)
            ], True)

    def attend_prefix(k):
        attend(k // halves, [
            (lambda j=j: kv[j, k, :, :HEAD], lambda j=j: kv[j, k, :, HEAD:], None)
            for j in range(4)
        ], False)

    depth = jnp.maximum(z, 3 - z)
    is_mine = (owner_mine == z).astype(jnp.int32)
    from_left = (owner_mine < z).astype(jnp.int32)
    in_lane_1 = (want == 1).astype(jnp.int32)

    def sent_on(lane):
        if lanes == 1:
            return ((owner_0 == z) | (owner_1 == z)).astype(jnp.int32)
        return ((owner_0, owner_1)[lane] == z).astype(jnp.int32)

    @pl.when(mid)
    def _():
        want_copy(jnp.where(z == 1, 0, 3)).wait_recv()

    edge_want = jnp.max(wanted[...])
    edge_owned = (jnp.where(edge_want == 1, owner_1, owner_0) == z).astype(jnp.int32)

    def step(i, carry):
        k_right = i - z

        @pl.when(mid & (k_right >= 0) & (k_right < chunks))
        def _():
            k = k_right

            @pl.when(z == 1)
            def _():
                right(0, k).wait_recv()
                for lane in range(lanes):
                    right_out[lane, k] = choose(sent_on(lane), own[k], right_in[0, k])
                    right(lane, k).start()

            @pl.when(z == 2)
            def _():
                got = None
                for lane in range(lanes):
                    right(lane, k).wait_recv()
                got = right_in[0, k]
                if lanes > 1:
                    got = choose(edge_want, right_in[1, k], got)
                right_out[0, k] = choose(edge_owned, own[k], got)
                right(0, k).start()

        k_left = i - (3 - z)

        @pl.when(mid & (k_left >= 0) & (k_left < chunks))
        def _():
            k = k_left

            @pl.when(z == 2)
            def _():
                left(0, k).wait_recv()
                for lane in range(lanes):
                    left_out[lane, k] = choose(sent_on(lane), own[k], left_in[0, k])
                    left(lane, k).start()

            @pl.when(z == 1)
            def _():
                for lane in range(lanes):
                    left(lane, k).wait_recv()
                got = left_in[0, k]
                if lanes > 1:
                    got = choose(edge_want, left_in[1, k], got)
                left_out[0, k] = choose(edge_owned, own[k], got)
                left(0, k).start()

        k_mine = i - depth

        @pl.when((k_mine >= 0) & (k_mine < chunks))
        def _():
            k = k_mine

            @pl.when(z == 0)
            def _():
                left(0, k).wait_recv()
                kv[0, k] = choose(is_mine, own[k], left_in[0, k])

            @pl.when(z == 3)
            def _():
                right(0, k).wait_recv()
                kv[0, k] = choose(is_mine, own[k], right_in[0, k])

            @pl.when(z == 1)
            def _():
                came = left_in[0, k]
                if lanes > 1:
                    came = choose(in_lane_1, left_in[1, k], came)
                came = choose(from_left, right_in[0, k], came)
                kv[0, k] = choose(is_mine, own[k], came)

            @pl.when(z == 2)
            def _():
                came = right_in[0, k]
                if lanes > 1:
                    came = choose(in_lane_1, right_in[1, k], came)
                came = choose(from_left, came, left_in[0, k])
                kv[0, k] = choose(is_mine, own[k], came)

            cross(k).start()
            core(k).start()

        k_cross = i - depth - 1

        @pl.when((k_cross >= 0) & (k_cross < chunks))
        def _():
            cross(k_cross).wait_recv()
            forward(k_cross).start()

        k_use = i - depth - 2

        @pl.when((k_use >= 0) & (k_use < chunks))
        def _():
            core(k_use).wait_recv()
            forward(k_use).wait_recv()
            attend_prefix(k_use)

        @pl.when(i == 1)
        def _():
            for c in suffix_copies(2):
                c.wait_recv()
            for c in suffix_copies(3):
                c.start()
            for j in (1, 3):
                for c in suffix_copies(j):
                    c.wait_recv()
            attend_suffix()

        return carry

    lax.fori_loop(0, chunks + depth + 2, step, 0)

    @pl.loop(0, heads * group_size)
    def _(head):
        col = pl.multiple_of(head * HEAD, HEAD)
        out[:, pl.ds(col, HEAD)] = (acc[head] / l_ref[head]).astype(out.dtype)

    for j in (1, 2, 3):
        for c in suffix_copies(j):
            c.wait_send()

    @pl.when((z == 0) | (z == 3))
    def _():
        want_copy(jnp.where(z == 0, 1, 2)).wait_send()

    @pl.loop(0, chunks)
    def _(k):
        core(k).wait_send()
        cross(k).wait_send()
        forward(k).wait_send()

        @pl.when(z < 3)
        def _():
            right(0, k).wait_send()

        @pl.when(z > 0)
        def _():
            left(0, k).wait_send()

        if lanes > 1:
            @pl.when(z == 1)
            def _():
                right(1, k).wait_send()

            @pl.when(z == 2)
            def _():
                left(1, k).wait_send()


def fused(lanes, owner, group_of, pages, queries, suffix, seg_row, pool):
    tokens, width = queries.shape
    heads = suffix.shape[1] // (2 * HEAD)
    q_heads = width // HEAD
    chunks = 2 * heads
    piece = (pages.shape[1] * pool.shape[1] // 2, 2 * HEAD)
    vmem, smem = pl.BlockSpec(memory_space=pltpu.VMEM), pl.BlockSpec(memory_space=pltpu.SMEM)
    dma = pltpu.SemaphoreType.DMA
    return pl.pallas_call(
        functools.partial(fused_kernel, lanes, heads, q_heads // heads),
        out_shape=jax.ShapeDtypeStruct((tokens, width), jnp.bfloat16),
        in_specs=[smem] * 3 + [vmem] * 4,
        out_specs=vmem,
        scratch_shapes=[
            pltpu.VMEM((chunks,) + piece, jnp.bfloat16),
            pltpu.VMEM((8, tokens), jnp.int32),
            pltpu.VMEM((tokens, HEAD), jnp.int32),
            pltpu.VMEM((8, HEAD), jnp.int32),
            pltpu.VMEM((8, HEAD), jnp.int32),
        ]
        + [pltpu.VMEM((lanes, chunks) + piece, jnp.bfloat16)] * 4
        + [
            pltpu.VMEM((4, chunks) + piece, jnp.bfloat16),
            pltpu.VMEM((3,) + suffix.shape, jnp.bfloat16),
            pltpu.VMEM((3, 8, tokens), jnp.int32),
            pltpu.VMEM((q_heads, tokens, HEAD), jnp.float32),
            pltpu.VMEM((q_heads, tokens, HEAD), jnp.float32),
            pltpu.VMEM((q_heads, tokens, HEAD), jnp.float32),
        ]
        + [dma((lanes, chunks))] * 4
        + [dma((chunks,))] * 6
        + [dma((3,))] * 4
        + [dma] * 2,
        compiler_params=pltpu.CompilerParams(
            collective_id=lanes, has_side_effects=True, vmem_limit_bytes=58 << 20
        ),
    )(owner, group_of, pages, queries, suffix, seg_row, pool)


def local_fused(queries, suffix_kv, suffix_seg, prefix_pool, page_table, owner, group_of):
    args = (owner, group_of, page_table, queries[0], suffix_kv[0], suffix_seg, prefix_pool[0])
    apart = (owner[0] < 2) != (owner[1] < 2)
    return lax.cond(
        apart, functools.partial(fused, 1), functools.partial(fused, 2), *args
    )[None]


def fits(mesh):
    return dict(mesh.shape) == {"group": 4, "seq": 4, "tensor": 2}


def solution(mesh):
    return jax.shard_map(
        local_fused if fits(mesh) else local,
        mesh=mesh,
        in_specs=(
            P("group", "seq", "tensor"),
            P("group", "seq", "tensor"),
            P("group", "seq"),
            P("group", "seq", None, "tensor"),
            P(None, "seq"),
            P(),
            P("group"),
        ),
        out_specs=P("group", "seq", "tensor"),
        check_vma=False,
    )
```

```python
import functools
import math

import jax
import jax.numpy as jnp
from jax import lax
from jax.experimental import pallas as pl
from jax.experimental.pallas import tpu as pltpu
from jax.sharding import PartitionSpec as P

HEAD = 128


NEG_FILL = -1e30


def broadcast(value, axis, root):
    mine = lax.axis_index(axis) == root
    return lax.psum(jnp.where(mine, value, jnp.zeros_like(value)), axis)


def absorb(carried, query_rows, key_block, valid):
    running_max, running_sum, accumulator = carried
    scale = 1.0 / math.sqrt(HEAD)
    key_rows = key_block[:, :, 0, :]
    value_rows = key_block[:, :, 1, :]
    scores = (
        jnp.einsum("thgd,khd->htgk", query_rows, key_rows, preferred_element_type=jnp.float32)
        * scale
    )
    if valid is not None:
        scores = jnp.where(valid[None, :, None, :], scores, NEG_FILL)
    new_max = jnp.maximum(running_max, jnp.max(scores, axis=-1, keepdims=True))
    weight = jnp.exp(scores - new_max)
    if valid is not None:
        weight = jnp.where(valid[None, :, None, :], weight, 0.0)
    factor = jnp.exp(running_max - new_max)
    running_sum = running_sum * factor + jnp.sum(weight, axis=-1, keepdims=True)
    accumulator = accumulator * factor + jnp.einsum(
        "htgk,khd->htgd",
        weight.astype(jnp.bfloat16),
        value_rows,
        preferred_element_type=jnp.float32,
    )
    return (new_max, running_sum, accumulator)


def sweep(carried, query_rows, kv_rows, mask_for):
    row_count = kv_rows.shape[0]
    block_rows = math.gcd(row_count, 1024)
    head_count = kv_rows.shape[1] // (2 * HEAD)

    def absorb_block(block_index, state_now):
        offset = block_index * block_rows
        key_block = lax.dynamic_slice_in_dim(kv_rows, offset, block_rows, 0).reshape(
            block_rows, head_count, 2, HEAD
        )
        return absorb(state_now, query_rows, key_block, mask_for(offset, block_rows))

    if row_count == block_rows:
        return absorb_block(0, carried)
    return lax.fori_loop(0, row_count // block_rows, absorb_block, carried)


def combine(earlier, later):
    new_max = jnp.maximum(earlier[0], later[0])
    scale_first = jnp.exp(earlier[0] - new_max)
    scale_second = jnp.exp(later[0] - new_max)
    return (
        new_max,
        earlier[1] * scale_first + later[1] * scale_second,
        earlier[2] * scale_first + later[2] * scale_second,
    )


def no_mask(offset, block_rows):
    return None


def local(queries, suffix_kv, suffix_seg, prefix_pool, page_table, owner, group_of):
    tokens = queries.shape[1]
    row_width = suffix_kv.shape[-1]
    head_count = row_width // (2 * HEAD)
    group_size = queries.shape[-1] // (head_count * HEAD)
    query_rows = queries[0].reshape(tokens, head_count, group_size, HEAD)
    page_pool = prefix_pool[0]
    my_group = group_of[0]
    held_shape = (page_table.shape[1] * page_pool.shape[1], row_width)

    def compact(slot_ids):
        return jnp.take(page_pool, slot_ids, axis=0).reshape(-1, row_width)

    def visit_group(request, held_pages):
        moved_pages = broadcast(compact(page_table[request]), "group", owner[request])
        return jnp.where(request == my_group, moved_pages, held_pages)

    prefix_rows = lax.fori_loop(
        0, page_table.shape[0], visit_group, jnp.zeros(held_shape, jnp.bfloat16)
    )
    fresh_state = (
        jnp.full((head_count, tokens, group_size, 1), NEG_FILL, jnp.float32),
        jnp.zeros((head_count, tokens, group_size, 1), jnp.float32),
        jnp.zeros((head_count, tokens, group_size, HEAD), jnp.float32),
    )
    before = sweep(
        fresh_state, query_rows, lax.all_gather(prefix_rows, "seq", axis=0, tiled=True), no_mask
    )
    first_row = lax.axis_index("seq") * tokens
    query_pos = first_row + jnp.arange(tokens, dtype=jnp.int32)
    query_seg = suffix_seg[0]
    first_index = jnp.int32(0)
    kv_rows = lax.all_gather(suffix_kv[0], "seq", axis=0, tiled=True)
    key_segments = lax.all_gather(suffix_seg[0], "seq", axis=0, tiled=True)

    def mask_for(offset, block_rows):
        block_seg = lax.dynamic_slice_in_dim(key_segments, offset, block_rows, 0)
        key_pos = first_index + offset + jnp.arange(block_rows, dtype=jnp.int32)
        return (block_seg[None, :] == query_seg[:, None]) & (key_pos[None, :] <= query_pos[:, None])

    combined = sweep(fresh_state, query_rows, kv_rows, mask_for)
    final_state = combine(before, combined)
    outcome = final_state[2] / final_state[1]
    return outcome.transpose(1, 0, 2, 3).reshape(1, tokens, -1).astype(jnp.bfloat16)

MESH = pl.DeviceIdType.MESH
EXP2_SCALE = math.log2(math.e) / math.sqrt(HEAD)


def choose(flag, first, second):
    return lax.select(flag != 0, first, second)


def fused_kernel(
    lanes, heads, group_size,
    owner, group_of, pages, queries, suffix, seg_row, pool,
    out,
    own, seg, qseg, wants, wanted,
    right_in, left_in, right_out, left_out, kv, sseg, m_ref, l_ref, acc,
    sem_right_s, sem_right_r, sem_left_s, sem_left_r,
    sem_core_s, sem_core_r, sem_x_s, sem_x_r, sem_f_s, sem_f_r,
    sem_seg_s, sem_seg_r, sem_want_s, sem_want_r,
):
    z = lax.axis_index("group")
    s = lax.axis_index("seq")
    chunks, rows = own.shape[:2]
    parts = chunks // heads
    tokens = queries.shape[0]
    partner = s + 1 - 2 * lax.rem(s, 2)
    across = lax.rem(s + 2, 4)
    across_partner = lax.rem(partner + 2, 4)
    mid = (z == 1) | (z == 2)

    owner_0, owner_1, want = owner[0], owner[1], group_of[0]
    owner_mine = jnp.where(want == 1, owner_1, owner_0)

    wanted[...] = jnp.zeros_like(wanted)
    barrier = pltpu.get_barrier_semaphore()
    for there in (partner, across):
        pl.semaphore_signal(barrier, inc=1, device_id={"seq": there}, device_id_type=MESH)

    @pl.when(z > 0)
    def _():
        pl.semaphore_signal(barrier, inc=1, device_id={"group": z - 1}, device_id_type=MESH)

    @pl.when(z < 3)
    def _():
        pl.semaphore_signal(barrier, inc=1, device_id={"group": z + 1}, device_id_type=MESH)

    wants[...] = jnp.broadcast_to(want, wants.shape)
    seg[...] = jnp.broadcast_to(seg_row[...], seg.shape)
    qseg[...] = jnp.broadcast_to(seg_row[...], (HEAD, tokens)).T

    owned = jnp.where(owner_1 == z, 1, 0)
    page = pool.shape[1]
    in_part = rows // page

    @pl.loop(0, pages.shape[1])
    def _(j):
        slot = pages[owned, j]
        place = pl.ds(pl.multiple_of(lax.rem(j, in_part) * page, page), page)
        for h in range(heads):
            own[h * parts + j // in_part, place, :] = pool[
                slot, :, h * 2 * HEAD : (h + 1) * 2 * HEAD
            ]

    pl.semaphore_wait(barrier, jnp.where(mid, 4, 3))

    def move(src, dst, send, recv, axis, there):
        return pltpu.make_async_remote_copy(
            src_ref=src, dst_ref=dst, send_sem=send, recv_sem=recv,
            device_id={axis: there}, device_id_type=MESH,
        )

    def right(lane, k, src=None):
        return move(
            right_out.at[lane, k] if src is None else src, right_in.at[lane, k],
            sem_right_s.at[lane, k], sem_right_r.at[lane, k], "group", lax.rem(z + 1, 4),
        )

    def left(lane, k, src=None):
        return move(
            left_out.at[lane, k] if src is None else src, left_in.at[lane, k],
            sem_left_s.at[lane, k], sem_left_r.at[lane, k], "group", lax.rem(z + 3, 4),
        )

    def core(e):
        return move(kv.at[0, e], kv.at[1, e], sem_core_s.at[e], sem_core_r.at[e], "seq", partner)

    def cross(e):
        return move(kv.at[0, e], kv.at[2, e], sem_x_s.at[e], sem_x_r.at[e], "seq", across)

    def forward(e):
        return move(kv.at[2, e], kv.at[3, e], sem_f_s.at[e], sem_f_r.at[e], "seq", partner)

    def seg_copy(slot):
        return move(
            seg if slot < 2 else sseg.at[1], sseg.at[slot], sem_seg_s.at[slot],
            sem_seg_r.at[slot], "seq", across if slot == 1 else partner,
        )

    def want_copy(there):
        return move(wants, wanted, sem_want_s, sem_want_r, "group", there)

    @pl.when((z == 0) | (z == 3))
    def _():
        want_copy(jnp.where(z == 0, 1, 2)).start()

    @pl.when(z == 0)
    def _():
        @pl.loop(0, chunks)
        def _(k):
            right(0, k, own.at[k]).start()

    @pl.when(z == 3)
    def _():
        @pl.loop(0, chunks)
        def _(k):
            left(0, k, own.at[k]).start()

    seg_copy(1).start()
    seg_copy(0).start()

    for h in range(heads):
        kv[0, h] = suffix[:, h * 2 * HEAD : (h + 1) * 2 * HEAD]
        cross(h).start()
        core(h).start()

    def attend(head, blocks, init):
        col = pl.multiple_of(head * HEAD, HEAD)
        q = queries[:, pl.ds(col, HEAD)]
        scores = []
        for keys, _, valid in blocks:
            sc = lax.dot_general(
                q, keys(), (((1,), (1,)), ((), ())), preferred_element_type=jnp.float32
            )
            if valid is not None:
                sc = jnp.where(valid, sc, NEG_FILL)
            scores.append(sc)
        top = jnp.max(scores[0], axis=1, keepdims=True)
        for sc in scores[1:]:
            top = jnp.maximum(top, jnp.max(sc, axis=1, keepdims=True))
        if not init:
            old = m_ref[head][:, :1]
            top = jnp.maximum(old, top)
            factor = jnp.exp2((old - top) * EXP2_SCALE)
        total, context = None, None
        for sc, (_, values, valid) in zip(scores, blocks):
            w = jnp.exp2((sc - top) * EXP2_SCALE)
            if valid is not None:
                w = jnp.where(valid, w, 0.0)
            part = jnp.sum(w, axis=1, keepdims=True)
            add = jnp.dot(w.astype(jnp.bfloat16), values(), preferred_element_type=jnp.float32)
            total = part if total is None else total + part
            context = add if context is None else context + add
        if not init:
            total = total + l_ref[head][:, :1] * factor
            context = context + acc[head] * factor
        m_ref[head] = jnp.broadcast_to(top, (tokens, HEAD))
        l_ref[head] = jnp.broadcast_to(total, (tokens, HEAD))
        acc[head] = context

    def attend_suffix(h):
        q_pos = s * tokens + lax.broadcasted_iota(jnp.int32, (tokens, tokens), 0)
        k_off = lax.broadcasted_iota(jnp.int32, (tokens, tokens), 1)
        q_seg = qseg[:, :1]

        def mask(seg_rows, origin):
            return (seg_rows == q_seg) & (origin * tokens + k_off <= q_pos)

        sources = (
            (seg, s), (sseg.at[0], partner), (sseg.at[1], across), (sseg.at[2], across_partner),
        )
        masks = [mask(sg[:1, :], origin) for sg, origin in sources]
        blocks = [
            (lambda j=j: kv[j, h, :, :HEAD], lambda j=j: kv[j, h, :, HEAD:], valid)
            for j, valid in enumerate(masks)
        ]

        @pl.loop(0, group_size)
        def _(i):
            attend(h * group_size + i, blocks, True)

    joined = 2
    share = group_size // joined

    def attend_prefix(u):
        first = heads + u // joined * joined
        head = u // parts * group_size + lax.rem(u, joined) * share

        def half(j, at):
            return kv[j, pl.ds(first, joined), :, at : at + HEAD].reshape(joined * rows, HEAD)

        blocks = [
            (lambda j=j: half(j, 0), lambda j=j: half(j, HEAD), None) for j in range(4)
        ]
        for i in range(share):
            attend(head + i, blocks, False)

    depth = jnp.maximum(z, 3 - z)
    is_mine = (owner_mine == z).astype(jnp.int32)
    from_left = (owner_mine < z).astype(jnp.int32)
    in_lane_1 = (want == 1).astype(jnp.int32)

    def sent_on(lane):
        if lanes == 1:
            return ((owner_0 == z) | (owner_1 == z)).astype(jnp.int32)
        return ((owner_0, owner_1)[lane] == z).astype(jnp.int32)

    @pl.when(mid)
    def _():
        want_copy(jnp.where(z == 1, 0, 3)).wait_recv()

    edge_want = jnp.max(wanted[...])
    edge_owned = (jnp.where(edge_want == 1, owner_1, owner_0) == z).astype(jnp.int32)

    def step(i, carry):
        k_right = i - z

        @pl.when(mid & (k_right >= 0) & (k_right < chunks))
        def _():
            k = k_right

            @pl.when(z == 1)
            def _():
                right(0, k).wait_recv()
                for lane in range(lanes):
                    right_out[lane, k] = choose(sent_on(lane), own[k], right_in[0, k])
                    right(lane, k).start()

            @pl.when(z == 2)
            def _():
                got = None
                for lane in range(lanes):
                    right(lane, k).wait_recv()
                got = right_in[0, k]
                if lanes > 1:
                    got = choose(edge_want, right_in[1, k], got)
                right_out[0, k] = choose(edge_owned, own[k], got)
                right(0, k).start()

        k_left = i - (3 - z)

        @pl.when(mid & (k_left >= 0) & (k_left < chunks))
        def _():
            k = k_left

            @pl.when(z == 2)
            def _():
                left(0, k).wait_recv()
                for lane in range(lanes):
                    left_out[lane, k] = choose(sent_on(lane), own[k], left_in[0, k])
                    left(lane, k).start()

            @pl.when(z == 1)
            def _():
                for lane in range(lanes):
                    left(lane, k).wait_recv()
                got = left_in[0, k]
                if lanes > 1:
                    got = choose(edge_want, left_in[1, k], got)
                left_out[0, k] = choose(edge_owned, own[k], got)
                left(0, k).start()

        k_mine = i - depth

        @pl.when((k_mine >= 0) & (k_mine < chunks))
        def _():
            k = k_mine

            @pl.when(z == 0)
            def _():
                left(0, k).wait_recv()
                kv[0, heads + k] = choose(is_mine, own[k], left_in[0, k])

            @pl.when(z == 3)
            def _():
                right(0, k).wait_recv()
                kv[0, heads + k] = choose(is_mine, own[k], right_in[0, k])

            @pl.when(z == 1)
            def _():
                came = left_in[0, k]
                if lanes > 1:
                    came = choose(in_lane_1, left_in[1, k], came)
                came = choose(from_left, right_in[0, k], came)
                kv[0, heads + k] = choose(is_mine, own[k], came)

            @pl.when(z == 2)
            def _():
                came = right_in[0, k]
                if lanes > 1:
                    came = choose(in_lane_1, right_in[1, k], came)
                came = choose(from_left, came, left_in[0, k])
                kv[0, heads + k] = choose(is_mine, own[k], came)

            cross(heads + k).start()
            core(heads + k).start()

        k_cross = i - depth - 1

        @pl.when((k_cross >= 0) & (k_cross < chunks))
        def _():
            cross(heads + k_cross).wait_recv()
            forward(heads + k_cross).start()

        @pl.when(i == 1)
        def _():
            seg_copy(1).wait_recv()
            seg_copy(2).start()
            seg_copy(0).wait_recv()
            seg_copy(2).wait_recv()

        @pl.when((i >= 1) & (i < 1 + heads))
        def _():
            cross(i - 1).wait_recv()
            forward(i - 1).start()

        @pl.when((i >= 2) & (i < 2 + heads))
        def _():
            core(i - 2).wait_recv()
            forward(i - 2).wait_recv()
            attend_suffix(i - 2)

        k_use = i - depth - 2

        @pl.when((k_use >= 0) & (k_use < chunks))
        def _():
            core(heads + k_use).wait_recv()
            forward(heads + k_use).wait_recv()

        u = k_use - (joined - 1)

        @pl.when((u >= 0) & (u < chunks))
        def _():
            attend_prefix(u)

        return carry

    lax.fori_loop(0, chunks + depth + 1 + joined, step, 0)

    @pl.loop(0, heads * group_size)
    def _(head):
        col = pl.multiple_of(head * HEAD, HEAD)
        out[:, pl.ds(col, HEAD)] = (acc[head] / l_ref[head]).astype(out.dtype)

    for slot in range(3):
        seg_copy(slot).wait_send()

    @pl.when((z == 0) | (z == 3))
    def _():
        want_copy(jnp.where(z == 0, 1, 2)).wait_send()

    @pl.loop(0, heads + chunks)
    def _(e):
        core(e).wait_send()
        cross(e).wait_send()
        forward(e).wait_send()

    @pl.loop(0, chunks)
    def _(k):
        @pl.when(z < 3)
        def _():
            right(0, k).wait_send()

        @pl.when(z > 0)
        def _():
            left(0, k).wait_send()

        if lanes > 1:
            @pl.when(z == 1)
            def _():
                right(1, k).wait_send()

            @pl.when(z == 2)
            def _():
                left(1, k).wait_send()


def fused(lanes, owner, group_of, pages, queries, suffix, seg_row, pool):
    tokens, width = queries.shape
    heads = suffix.shape[1] // (2 * HEAD)
    q_heads = width // HEAD
    chunks = pages.shape[1] * pool.shape[1] // tokens * heads
    piece = (tokens, 2 * HEAD)
    vmem, smem = pl.BlockSpec(memory_space=pltpu.VMEM), pl.BlockSpec(memory_space=pltpu.SMEM)
    dma = pltpu.SemaphoreType.DMA
    return pl.pallas_call(
        functools.partial(fused_kernel, lanes, heads, q_heads // heads),
        out_shape=jax.ShapeDtypeStruct((tokens, width), jnp.bfloat16),
        in_specs=[smem] * 3 + [vmem] * 4,
        out_specs=vmem,
        scratch_shapes=[
            pltpu.VMEM((chunks,) + piece, jnp.bfloat16),
            pltpu.VMEM((8, tokens), jnp.int32),
            pltpu.VMEM((tokens, HEAD), jnp.int32),
            pltpu.VMEM((8, HEAD), jnp.int32),
            pltpu.VMEM((8, HEAD), jnp.int32),
        ]
        + [pltpu.VMEM((lanes, chunks) + piece, jnp.bfloat16)] * 4
        + [
            pltpu.VMEM((4, heads + chunks) + piece, jnp.bfloat16),
            pltpu.VMEM((3, 8, tokens), jnp.int32),
            pltpu.VMEM((q_heads, tokens, HEAD), jnp.float32),
            pltpu.VMEM((q_heads, tokens, HEAD), jnp.float32),
            pltpu.VMEM((q_heads, tokens, HEAD), jnp.float32),
        ]
        + [dma((lanes, chunks))] * 4
        + [dma((heads + chunks,))] * 6
        + [dma((3,))] * 2
        + [dma] * 2,
        compiler_params=pltpu.CompilerParams(
            collective_id=lanes, has_side_effects=True, vmem_limit_bytes=58 << 20
        ),
    )(owner, group_of, pages, queries, suffix, seg_row, pool)


def local_fused(queries, suffix_kv, suffix_seg, prefix_pool, page_table, owner, group_of):
    args = (owner, group_of, page_table, queries[0], suffix_kv[0], suffix_seg, prefix_pool[0])
    apart = (owner[0] < 2) != (owner[1] < 2)
    return lax.cond(
        apart, functools.partial(fused, 1), functools.partial(fused, 2), *args
    )[None]


def fits(mesh):
    return dict(mesh.shape) == {"group": 4, "seq": 4, "tensor": 2}


def solution(mesh):
    return jax.shard_map(
        local_fused if fits(mesh) else local,
        mesh=mesh,
        in_specs=(
            P("group", "seq", "tensor"),
            P("group", "seq", "tensor"),
            P("group", "seq"),
            P("group", "seq", None, "tensor"),
            P(None, "seq"),
            P(),
            P("group"),
        ),
        out_specs=P("group", "seq", "tensor"),
        check_vma=False,
    )
```

```python
import functools
import math

import jax
import jax.numpy as jnp
from jax import lax
from jax.experimental import pallas as pl
from jax.experimental.pallas import tpu as pltpu
from jax.sharding import PartitionSpec as P

HEAD = 128


NEG_FILL = -1e30


def broadcast(value, axis, root):
    mine = lax.axis_index(axis) == root
    return lax.psum(jnp.where(mine, value, jnp.zeros_like(value)), axis)


def absorb(carried, query_rows, key_block, valid):
    running_max, running_sum, accumulator = carried
    scale = 1.0 / math.sqrt(HEAD)
    key_rows = key_block[:, :, 0, :]
    value_rows = key_block[:, :, 1, :]
    scores = (
        jnp.einsum("thgd,khd->htgk", query_rows, key_rows, preferred_element_type=jnp.float32)
        * scale
    )
    if valid is not None:
        scores = jnp.where(valid[None, :, None, :], scores, NEG_FILL)
    new_max = jnp.maximum(running_max, jnp.max(scores, axis=-1, keepdims=True))
    weight = jnp.exp(scores - new_max)
    if valid is not None:
        weight = jnp.where(valid[None, :, None, :], weight, 0.0)
    factor = jnp.exp(running_max - new_max)
    running_sum = running_sum * factor + jnp.sum(weight, axis=-1, keepdims=True)
    accumulator = accumulator * factor + jnp.einsum(
        "htgk,khd->htgd",
        weight.astype(jnp.bfloat16),
        value_rows,
        preferred_element_type=jnp.float32,
    )
    return (new_max, running_sum, accumulator)


def sweep(carried, query_rows, kv_rows, mask_for):
    row_count = kv_rows.shape[0]
    block_rows = math.gcd(row_count, 1024)
    head_count = kv_rows.shape[1] // (2 * HEAD)

    def absorb_block(block_index, state_now):
        offset = block_index * block_rows
        key_block = lax.dynamic_slice_in_dim(kv_rows, offset, block_rows, 0).reshape(
            block_rows, head_count, 2, HEAD
        )
        return absorb(state_now, query_rows, key_block, mask_for(offset, block_rows))

    if row_count == block_rows:
        return absorb_block(0, carried)
    return lax.fori_loop(0, row_count // block_rows, absorb_block, carried)


def combine(earlier, later):
    new_max = jnp.maximum(earlier[0], later[0])
    scale_first = jnp.exp(earlier[0] - new_max)
    scale_second = jnp.exp(later[0] - new_max)
    return (
        new_max,
        earlier[1] * scale_first + later[1] * scale_second,
        earlier[2] * scale_first + later[2] * scale_second,
    )


def no_mask(offset, block_rows):
    return None


def local(queries, suffix_kv, suffix_seg, prefix_pool, page_table, owner, group_of):
    tokens = queries.shape[1]
    row_width = suffix_kv.shape[-1]
    head_count = row_width // (2 * HEAD)
    group_size = queries.shape[-1] // (head_count * HEAD)
    query_rows = queries[0].reshape(tokens, head_count, group_size, HEAD)
    page_pool = prefix_pool[0]
    my_group = group_of[0]
    held_shape = (page_table.shape[1] * page_pool.shape[1], row_width)

    def compact(slot_ids):
        return jnp.take(page_pool, slot_ids, axis=0).reshape(-1, row_width)

    def visit_group(request, held_pages):
        moved_pages = broadcast(compact(page_table[request]), "group", owner[request])
        return jnp.where(request == my_group, moved_pages, held_pages)

    prefix_rows = lax.fori_loop(
        0, page_table.shape[0], visit_group, jnp.zeros(held_shape, jnp.bfloat16)
    )
    fresh_state = (
        jnp.full((head_count, tokens, group_size, 1), NEG_FILL, jnp.float32),
        jnp.zeros((head_count, tokens, group_size, 1), jnp.float32),
        jnp.zeros((head_count, tokens, group_size, HEAD), jnp.float32),
    )
    before = sweep(
        fresh_state, query_rows, lax.all_gather(prefix_rows, "seq", axis=0, tiled=True), no_mask
    )
    first_row = lax.axis_index("seq") * tokens
    query_pos = first_row + jnp.arange(tokens, dtype=jnp.int32)
    query_seg = suffix_seg[0]
    first_index = jnp.int32(0)
    kv_rows = lax.all_gather(suffix_kv[0], "seq", axis=0, tiled=True)
    key_segments = lax.all_gather(suffix_seg[0], "seq", axis=0, tiled=True)

    def mask_for(offset, block_rows):
        block_seg = lax.dynamic_slice_in_dim(key_segments, offset, block_rows, 0)
        key_pos = first_index + offset + jnp.arange(block_rows, dtype=jnp.int32)
        return (block_seg[None, :] == query_seg[:, None]) & (key_pos[None, :] <= query_pos[:, None])

    combined = sweep(fresh_state, query_rows, kv_rows, mask_for)
    final_state = combine(before, combined)
    outcome = final_state[2] / final_state[1]
    return outcome.transpose(1, 0, 2, 3).reshape(1, tokens, -1).astype(jnp.bfloat16)

MESH = pl.DeviceIdType.MESH
HOP = 2
SPLIT = 1
EXP2_SCALE = math.log2(math.e) / math.sqrt(HEAD)


def choose(flag, first, second):
    return lax.select(flag != 0, first, second)


def fused_kernel(
    lanes, heads, group_size,
    owner, group_of, pages, queries, suffix, seg_row, pool,
    out,
    own, seg, qseg, wants, wanted,
    right_in, left_in, right_out, left_out, kv, sseg, m_ref, l_ref, acc,
    sem_right_s, sem_right_r, sem_left_s, sem_left_r,
    sem_core_s, sem_core_r, sem_x_s, sem_x_r, sem_f_s, sem_f_r,
    sem_seg_s, sem_seg_r, sem_want_s, sem_want_r,
):
    z = lax.axis_index("group")
    s = lax.axis_index("seq")
    chunks, rows = own.shape[:2]
    parts = chunks // heads
    tokens = queries.shape[0]
    entries = heads * SPLIT
    partner = s + 1 - 2 * lax.rem(s, 2)
    across = lax.rem(s + 2, 4)
    across_partner = lax.rem(partner + 2, 4)
    mid = (z == 1) | (z == 2)

    owner_0, owner_1, want = owner[0], owner[1], group_of[0]
    owner_mine = jnp.where(want == 1, owner_1, owner_0)

    wanted[...] = jnp.zeros_like(wanted)
    barrier = pltpu.get_barrier_semaphore()
    for there in (partner, across):
        pl.semaphore_signal(barrier, inc=1, device_id={"seq": there}, device_id_type=MESH)

    @pl.when(z > 0)
    def _():
        pl.semaphore_signal(barrier, inc=1, device_id={"group": z - 1}, device_id_type=MESH)

    @pl.when(z < 3)
    def _():
        pl.semaphore_signal(barrier, inc=1, device_id={"group": z + 1}, device_id_type=MESH)

    wants[...] = jnp.broadcast_to(want, wants.shape)
    seg[...] = jnp.broadcast_to(seg_row[...], seg.shape)
    qseg[...] = jnp.broadcast_to(seg_row[...], (HEAD, tokens)).T

    owned = jnp.where(owner_1 == z, 1, 0)
    page = pool.shape[1]
    in_part = rows // page

    @pl.loop(0, pages.shape[1])
    def _(j):
        slot = pages[owned, j]
        place = pl.ds(pl.multiple_of(lax.rem(j, in_part) * page, page), page)
        for h in range(heads):
            own[h * parts + j // in_part, place, :] = pool[
                slot, :, h * 2 * HEAD : (h + 1) * 2 * HEAD
            ]

    pl.semaphore_wait(barrier, jnp.where(mid, 4, 3))

    def move(src, dst, send, recv, axis, there):
        return pltpu.make_async_remote_copy(
            src_ref=src, dst_ref=dst, send_sem=send, recv_sem=recv,
            device_id={axis: there}, device_id_type=MESH,
        )

    def right(lane, k, src=None):
        return move(
            right_out.at[lane, k] if src is None else src, right_in.at[lane, k],
            sem_right_s.at[lane, k], sem_right_r.at[lane, k], "group", lax.rem(z + 1, 4),
        )

    def left(lane, k, src=None):
        return move(
            left_out.at[lane, k] if src is None else src, left_in.at[lane, k],
            sem_left_s.at[lane, k], sem_left_r.at[lane, k], "group", lax.rem(z + 3, 4),
        )

    def core(e):
        return move(kv.at[0, e], kv.at[1, e], sem_core_s.at[e], sem_core_r.at[e], "seq", partner)

    def cross(e):
        return move(kv.at[0, e], kv.at[2, e], sem_x_s.at[e], sem_x_r.at[e], "seq", across)

    def forward(e):
        return move(kv.at[2, e], kv.at[3, e], sem_f_s.at[e], sem_f_r.at[e], "seq", partner)

    def seg_copy(slot):
        return move(
            seg if slot < 2 else sseg.at[1], sseg.at[slot], sem_seg_s.at[slot],
            sem_seg_r.at[slot], "seq", across if slot == 1 else partner,
        )

    def want_copy(there):
        return move(wants, wanted, sem_want_s, sem_want_r, "group", there)

    @pl.when((z == 0) | (z == 3))
    def _():
        want_copy(jnp.where(z == 0, 1, 2)).start()

    @pl.when(z == 0)
    def _():
        @pl.loop(0, chunks)
        def _(k):
            right(0, k, own.at[k]).start()

    @pl.when(z == 3)
    def _():
        @pl.loop(0, chunks)
        def _(k):
            left(0, k, own.at[k]).start()

    seg_copy(1).start()
    seg_copy(0).start()

    for e in range(entries):
        h, top = e // SPLIT, e % SPLIT * rows
        kv[0, e] = suffix[top : top + rows, h * 2 * HEAD : (h + 1) * 2 * HEAD]
        cross(e).start()
        core(e).start()

    def attend(head, blocks, init):
        col = pl.multiple_of(head * HEAD, HEAD)
        q = queries[:, pl.ds(col, HEAD)]
        scores = []
        for keys, _, valid in blocks:
            sc = lax.dot_general(
                q, keys(), (((1,), (1,)), ((), ())), preferred_element_type=jnp.float32
            )
            if valid is not None:
                sc = jnp.where(valid, sc, NEG_FILL)
            scores.append(sc)
        top = jnp.max(scores[0], axis=1, keepdims=True)
        for sc in scores[1:]:
            top = jnp.maximum(top, jnp.max(sc, axis=1, keepdims=True))
        if not init:
            old = m_ref[head][:, :1]
            top = jnp.maximum(old, top)
            factor = jnp.exp2((old - top) * EXP2_SCALE)
        total, context = None, None
        for sc, (_, values, valid) in zip(scores, blocks):
            w = jnp.exp2((sc - top) * EXP2_SCALE)
            if valid is not None:
                w = jnp.where(valid, w, 0.0)
            part = jnp.sum(w, axis=1, keepdims=True)
            add = jnp.dot(w.astype(jnp.bfloat16), values(), preferred_element_type=jnp.float32)
            total = part if total is None else total + part
            context = add if context is None else context + add
        if not init:
            total = total + l_ref[head][:, :1] * factor
            context = context + acc[head] * factor
        m_ref[head] = jnp.broadcast_to(top, (tokens, HEAD))
        l_ref[head] = jnp.broadcast_to(total, (tokens, HEAD))
        acc[head] = context

    def attend_suffix(h):
        q_pos = s * tokens + lax.broadcasted_iota(jnp.int32, (tokens, tokens), 0)
        k_off = lax.broadcasted_iota(jnp.int32, (tokens, tokens), 1)
        q_seg = qseg[:, :1]

        def mask(seg_rows, origin):
            return (seg_rows == q_seg) & (origin * tokens + k_off <= q_pos)

        sources = (
            (seg, s), (sseg.at[0], partner), (sseg.at[1], across), (sseg.at[2], across_partner),
        )
        masks = [mask(sg[:1, :], origin) for sg, origin in sources]
        def half(j, at):
            return kv[j, pl.ds(h * SPLIT, SPLIT), :, at : at + HEAD].reshape(tokens, HEAD)

        blocks = [
            (lambda j=j: half(j, 0), lambda j=j: half(j, HEAD), valid)
            for j, valid in enumerate(masks)
        ]

        @pl.loop(0, group_size)
        def _(i):
            attend(h * group_size + i, blocks, True)

    joined = 2 * SPLIT
    share = group_size // joined

    def attend_prefix(u):
        first = entries + u // joined * joined
        head = u // parts * group_size + lax.rem(u, joined) * share

        def half(j, at):
            return kv[j, pl.ds(first, joined), :, at : at + HEAD].reshape(joined * rows, HEAD)

        blocks = [
            (lambda j=j: half(j, 0), lambda j=j: half(j, HEAD), None) for j in range(4)
        ]
        for i in range(share):
            attend(head + i, blocks, False)

    depth = HOP * jnp.maximum(z, 3 - z)
    is_mine = (owner_mine == z).astype(jnp.int32)
    from_left = (owner_mine < z).astype(jnp.int32)
    in_lane_1 = (want == 1).astype(jnp.int32)

    def sent_on(lane):
        if lanes == 1:
            return ((owner_0 == z) | (owner_1 == z)).astype(jnp.int32)
        return ((owner_0, owner_1)[lane] == z).astype(jnp.int32)

    @pl.when(mid)
    def _():
        want_copy(jnp.where(z == 1, 0, 3)).wait_recv()

    edge_want = jnp.max(wanted[...])
    edge_owned = (jnp.where(edge_want == 1, owner_1, owner_0) == z).astype(jnp.int32)

    def step(i, carry):
        k_right = i - HOP * z

        @pl.when(mid & (k_right >= 0) & (k_right < chunks))
        def _():
            k = k_right

            @pl.when(z == 1)
            def _():
                right(0, k).wait_recv()
                for lane in range(lanes):
                    right_out[lane, k] = choose(sent_on(lane), own[k], right_in[0, k])
                    right(lane, k).start()

            @pl.when(z == 2)
            def _():
                got = None
                for lane in range(lanes):
                    right(lane, k).wait_recv()
                got = right_in[0, k]
                if lanes > 1:
                    got = choose(edge_want, right_in[1, k], got)
                right_out[0, k] = choose(edge_owned, own[k], got)
                right(0, k).start()

        k_left = i - HOP * (3 - z)

        @pl.when(mid & (k_left >= 0) & (k_left < chunks))
        def _():
            k = k_left

            @pl.when(z == 2)
            def _():
                left(0, k).wait_recv()
                for lane in range(lanes):
                    left_out[lane, k] = choose(sent_on(lane), own[k], left_in[0, k])
                    left(lane, k).start()

            @pl.when(z == 1)
            def _():
                for lane in range(lanes):
                    left(lane, k).wait_recv()
                got = left_in[0, k]
                if lanes > 1:
                    got = choose(edge_want, left_in[1, k], got)
                left_out[0, k] = choose(edge_owned, own[k], got)
                left(0, k).start()

        k_mine = i - depth

        @pl.when((k_mine >= 0) & (k_mine < chunks))
        def _():
            k = k_mine

            @pl.when(z == 0)
            def _():
                left(0, k).wait_recv()
                kv[0, entries + k] = choose(is_mine, own[k], left_in[0, k])

            @pl.when(z == 3)
            def _():
                right(0, k).wait_recv()
                kv[0, entries + k] = choose(is_mine, own[k], right_in[0, k])

            @pl.when(z == 1)
            def _():
                came = left_in[0, k]
                if lanes > 1:
                    came = choose(in_lane_1, left_in[1, k], came)
                came = choose(from_left, right_in[0, k], came)
                kv[0, entries + k] = choose(is_mine, own[k], came)

            @pl.when(z == 2)
            def _():
                came = right_in[0, k]
                if lanes > 1:
                    came = choose(in_lane_1, right_in[1, k], came)
                came = choose(from_left, came, left_in[0, k])
                kv[0, entries + k] = choose(is_mine, own[k], came)

            cross(entries + k).start()
            core(entries + k).start()

        k_cross = i - depth - HOP

        @pl.when((k_cross >= 0) & (k_cross < chunks))
        def _():
            cross(entries + k_cross).wait_recv()
            forward(entries + k_cross).start()

        @pl.when(i == 1)
        def _():
            seg_copy(1).wait_recv()
            seg_copy(2).start()
            seg_copy(0).wait_recv()
            seg_copy(2).wait_recv()

        @pl.when((i >= 1) & (i < 1 + entries))
        def _():
            cross(i - 1).wait_recv()
            forward(i - 1).start()

        e = i - 1 - HOP

        @pl.when((e >= 0) & (e < entries))
        def _():
            core(e).wait_recv()
            forward(e).wait_recv()

            @pl.when(lax.rem(e, SPLIT) == SPLIT - 1)
            def _():
                attend_suffix(e // SPLIT)

        k_use = i - depth - HOP - 1

        @pl.when((k_use >= 0) & (k_use < chunks))
        def _():
            core(entries + k_use).wait_recv()
            forward(entries + k_use).wait_recv()

        u = k_use - (joined - 1)

        @pl.when((u >= 0) & (u < chunks))
        def _():
            attend_prefix(u)

        return carry

    lax.fori_loop(0, chunks + depth + HOP + joined, step, 0)

    @pl.loop(0, heads * group_size)
    def _(head):
        col = pl.multiple_of(head * HEAD, HEAD)
        out[:, pl.ds(col, HEAD)] = (acc[head] / l_ref[head]).astype(out.dtype)

    for slot in range(3):
        seg_copy(slot).wait_send()

    @pl.when((z == 0) | (z == 3))
    def _():
        want_copy(jnp.where(z == 0, 1, 2)).wait_send()

    @pl.loop(0, entries + chunks)
    def _(e):
        core(e).wait_send()
        cross(e).wait_send()
        forward(e).wait_send()

    @pl.loop(0, chunks)
    def _(k):
        @pl.when(z < 3)
        def _():
            right(0, k).wait_send()

        @pl.when(z > 0)
        def _():
            left(0, k).wait_send()

        if lanes > 1:
            @pl.when(z == 1)
            def _():
                right(1, k).wait_send()

            @pl.when(z == 2)
            def _():
                left(1, k).wait_send()


def fused(lanes, owner, group_of, pages, queries, suffix, seg_row, pool):
    tokens, width = queries.shape
    heads = suffix.shape[1] // (2 * HEAD)
    q_heads = width // HEAD
    piece = (tokens // SPLIT, 2 * HEAD)
    chunks = pages.shape[1] * pool.shape[1] // piece[0] * heads
    vmem, smem = pl.BlockSpec(memory_space=pltpu.VMEM), pl.BlockSpec(memory_space=pltpu.SMEM)
    dma = pltpu.SemaphoreType.DMA
    return pl.pallas_call(
        functools.partial(fused_kernel, lanes, heads, q_heads // heads),
        out_shape=jax.ShapeDtypeStruct((tokens, width), jnp.bfloat16),
        in_specs=[smem] * 3 + [vmem] * 4,
        out_specs=vmem,
        scratch_shapes=[
            pltpu.VMEM((chunks,) + piece, jnp.bfloat16),
            pltpu.VMEM((8, tokens), jnp.int32),
            pltpu.VMEM((tokens, HEAD), jnp.int32),
            pltpu.VMEM((8, HEAD), jnp.int32),
            pltpu.VMEM((8, HEAD), jnp.int32),
        ]
        + [pltpu.VMEM((lanes, chunks) + piece, jnp.bfloat16)] * 4
        + [
            pltpu.VMEM((4, heads * SPLIT + chunks) + piece, jnp.bfloat16),
            pltpu.VMEM((3, 8, tokens), jnp.int32),
            pltpu.VMEM((q_heads, tokens, HEAD), jnp.float32),
            pltpu.VMEM((q_heads, tokens, HEAD), jnp.float32),
            pltpu.VMEM((q_heads, tokens, HEAD), jnp.float32),
        ]
        + [dma((lanes, chunks))] * 4
        + [dma((heads * SPLIT + chunks,))] * 6
        + [dma((3,))] * 2
        + [dma] * 2,
        compiler_params=pltpu.CompilerParams(
            collective_id=lanes, has_side_effects=True, vmem_limit_bytes=58 << 20
        ),
    )(owner, group_of, pages, queries, suffix, seg_row, pool)


def local_fused(queries, suffix_kv, suffix_seg, prefix_pool, page_table, owner, group_of):
    args = (owner, group_of, page_table, queries[0], suffix_kv[0], suffix_seg, prefix_pool[0])
    apart = (owner[0] < 2) != (owner[1] < 2)
    return lax.cond(
        apart, functools.partial(fused, 1), functools.partial(fused, 2), *args
    )[None]


def fits(mesh):
    return dict(mesh.shape) == {"group": 4, "seq": 4, "tensor": 2}


def solution(mesh):
    return jax.shard_map(
        local_fused if fits(mesh) else local,
        mesh=mesh,
        in_specs=(
            P("group", "seq", "tensor"),
            P("group", "seq", "tensor"),
            P("group", "seq"),
            P("group", "seq", None, "tensor"),
            P(None, "seq"),
            P(),
            P("group"),
        ),
        out_specs=P("group", "seq", "tensor"),
        check_vma=False,
    )
```
